32 devices in a mesh: group: 2 (over x), tensor: 8 (over z, y), dp: 2 (over core).
Axes of the slice: x: 2, y: 2, z: 4, core: 2. Of those that a mesh axis runs over, the one named last changes fastest.
Arguments:
- features: bfloat16 [512, 8192], P(('group', 'dp'), 'tensor'), parts along dimension 0, may hold values from -64 to 64
- cotangent: bfloat16 [512, 8192], P(('group', 'dp'), 'tensor'), parts along dimension 0, may hold values from -64 to 64
- token_tenant: int32 [512], P(('group', 'dp')), parts along dimension 0, may hold values from 0 to 15
- owner_device: int32 [32], P('group'), parts along dimension 0, may hold values from 0 to 15, each once
- frozen_weight: bfloat16 [8192, 8192], P('tensor'), may hold values from -0.09375 to 0.09375
- adapter_down: bfloat16 [32, 16, 8192], P('group', None, 'tensor'), parts along dimension 0, may hold values from -0.0625 to 0.0625
- adapter_up: bfloat16 [32, 16, 8192], P('group', None, 'tensor'), parts along dimension 0, may hold values from -0.29882812 to 0.29882812
- momentum_down: float32 [32, 16, 8192], P(('group', 'tensor', 'dp')), parts along dimension 0, may hold values from -12 to 12
- momentum_up: float32 [32, 16, 8192], P(('group', 'tensor', 'dp')), parts along dimension 0, may hold values from -3 to 3
- variance_down: float32 [32, 16, 8192], P(('group', 'tensor', 'dp')), parts along dimension 0, may hold values from 0.3 to 3
- variance_up: float32 [32, 16, 8192], P(('group', 'tensor', 'dp')), parts along dimension 0, may hold values from 0.02 to 0.2
Outputs:
- projected: bfloat16 [512, 8192], P(('group', 'dp'), 'tensor'), parts along dimension 0
- updated_down: bfloat16 [32, 16, 8192], P('group', None, 'tensor'), parts along dimension 0
- updated_up: bfloat16 [32, 16, 8192], P('group', None, 'tensor'), parts along dimension 0
- mean_down: float32 [32, 16, 8192], P(('group', 'tensor', 'dp')), parts along dimension 0
- mean_up: float32 [32, 16, 8192], P(('group', 'tensor', 'dp')), parts along dimension 0
- power_down: float32 [32, 16, 8192], P(('group', 'tensor', 'dp')), parts along dimension 0
- power_up: float32 [32, 16, 8192], P(('group', 'tensor', 'dp')), parts along dimension 0
The draws below stay inside these ranges and needn't reach their ends.
There are 2 independent parts, one for each index of `group`. The reference program is written for one: setup_inputs(seed, part) draws one part's arguments, and reference() takes and returns one part's arrays. A program takes and returns all parts, laid end to end along the dimension named above; an argument that names none is the same for every part. Nothing has to cross between parts.
Inputs may be any that keep to these rules, and one draw needn't show every extreme that they name: Tenant t belongs to the device whose index along tensor+dp (dp fastest) is owner_device[t]; every index appears once.
All inputs are finite; a program needn't handle non-finite values.
Results may differ from the reference program's by a relative error of at most 0.0014.
The reference program's roundings to bfloat16 on the way count: a program that leaves them out, or rounds other values in their place, can miss the bound.
Values sent between devices are 32-bit elements; how exact they have to be, the bound alone decides.
A program may use at most 128 MiB of HBM per device.

```python
import math
import jax
import jax.numpy as jnp
import numpy as np
from jax import lax

D = 8192
RANK = 16
TEN = 16
TOKENS = 256


def rough_rows(key, height, breadth):
    subkeys = jax.random.split(key, 3)
    position = jnp.arange(breadth, dtype=jnp.float32) / max(breadth - 1, 1)
    rough_noise = jnp.clip(jax.random.normal(subkeys[0], (height, breadth), jnp.float32), -4.0, 4.0)
    column_trend = jnp.exp(jnp.log(3.0) * position) / 1.7
    row_scale = jnp.exp(jax.random.uniform(subkeys[1], (height, 1), jnp.float32, jnp.log(0.3), jnp.log(3.0)))
    col_scale = column_trend * jnp.exp(jax.random.uniform(subkeys[2], (breadth,), jnp.float32, jnp.log(0.3), jnp.log(3.0)))
    return jnp.clip(rough_noise * row_scale * col_scale[None, :], -64.0, 64.0)


def draw_features(key, part):
    return rough_rows(jax.random.fold_in(key, 11), TOKENS, D).astype(jnp.bfloat16)


def draw_cotangent(key, part):
    return rough_rows(jax.random.fold_in(key, 23), TOKENS, D).astype(jnp.bfloat16)


def set_ends(drawn, stream_key, least, top_value):
    place = [jax.random.randint(jax.random.fold_in(stream_key, axis), (), 0, length) for axis, length in enumerate(drawn.shape)]
    longest = drawn.shape.index(max(drawn.shape))
    neighbour = place[:longest] + [(place[longest] + 1) % drawn.shape[longest]] + place[longest + 1:]
    return drawn.at[tuple(place)].set(least).at[tuple(neighbour)].set(top_value)


def spiked(array, rng, source, target, shards_of, factor):
    def block_of(axis_at):
        return (jnp.arange(array.shape[axis_at]) // (array.shape[axis_at] // shards_of)).reshape((-1,) + (1,) * (array.ndim - 1 - axis_at))

    one_side = jax.random.permutation(rng, shards_of)[block_of(target)]
    other_side = (block_of(target) + shards_of // 2) % shards_of
    return jnp.where((block_of(source) == one_side) | (block_of(source) == other_side), factor * array, array)


def block_levels(key, extent, shards, smallest, largest):
    loudness = 1.0
    for dim, blocks in shards:
        draws = jax.random.uniform(jax.random.fold_in(jax.random.fold_in(key, 6), dim), (blocks,), jnp.float32, smallest / len(shards), largest / len(shards))
        loudness = loudness * jnp.repeat(jnp.exp(draws), extent[dim] // blocks).reshape((-1,) + (1,) * (len(extent) - 1 - dim))
    return loudness


def rank_bounds(number_of, skew):
    loads = [(1 << 20) // math.isqrt(rank ** skew) + 1 for rank in range(1, number_of + 1)]
    scale = 1 + sum(loads) // (1 << 30)
    return np.cumsum(np.array([max(1, weight // scale) for weight in loads]))


def ranked_ids(own_key, shape, count, slope):
    table = rank_bounds(count, slope)
    lot = jax.random.randint(jax.random.fold_in(own_key, 1), shape, 0, int(table[count - 1]))
    grade = jnp.searchsorted(jnp.asarray(table, jnp.int32), lot, side="right")
    return jax.random.permutation(jax.random.fold_in(own_key, 2), count)[grade].astype(jnp.int32)


def scatter_about(stream_key, extent, deviation, bound, cuts=(), held_as=jnp.bfloat16):
    loudness = block_levels(stream_key, extent, cuts, -0.22, 0.18) if cuts else 1.0
    array = jax.random.normal(stream_key, extent, jnp.float32) * deviation * loudness
    return jnp.minimum(jnp.maximum(array, -bound), bound).astype(held_as)


def noise_with(rng, dims, scale, most, pieces, heavy, kind=jnp.bfloat16):
    drawn = scale * jax.random.normal(rng, dims, jnp.float32)
    if pieces:
        drawn = drawn * block_levels(rng, dims, pieces, -0.22, 0.18)
    return jnp.clip(spiked(drawn, jax.random.fold_in(rng, 3), *heavy), -most, most).astype(kind)


def setup_inputs(seed: int = 0, part: int = 0) -> dict:
    splits = jax.random.split(jax.random.key(seed), 12)
    own_keys = jax.random.split(jax.random.fold_in(splits[11], part), 12)
    features = draw_features(jax.random.fold_in(jax.random.fold_in(splits[11], part), 71), part)
    cotangent = draw_cotangent(jax.random.fold_in(jax.random.fold_in(splits[11], part), 71), part)
    token_tenant = set_ends(ranked_ids(own_keys[2], (TOKENS,), TEN, 2), jax.random.fold_in(own_keys[2], 3), 0, TEN - 1).astype(jnp.int32)
    owner_device = jax.random.permutation(own_keys[3], TEN).astype(jnp.int32)
    frozen_weight = noise_with(splits[4], (D, D), D ** -0.5, 0.09375, ((0, 8),), (0, 1, 8, 2.0))
    adapter_down = scatter_about(own_keys[5], (TEN, RANK, D), D ** -0.5, 0.0625, ((2, 8),))
    adapter_up = scatter_about(own_keys[6], (TEN, RANK, D), 0.05, 0.29882812, ((2, 8),))
    momentum_down = scatter_about(own_keys[7], (TEN, RANK, D), 2.0, 12.0, ((0, 16),), jnp.float32)
    momentum_up = scatter_about(own_keys[8], (TEN, RANK, D), 0.5, 3.0, ((0, 16),), jnp.float32)
    variance_down = jnp.clip(jnp.exp(math.log(3.0) - 2.3025851 * jax.random.uniform(own_keys[9], (TEN, RANK, D), jnp.float32) ** block_levels(own_keys[9], (TEN, RANK, D), ((0, 16),), -0.2, 0.2)), 0.3, 3.0)
    variance_up = jnp.clip(jnp.exp(math.log(0.2) - 2.3025851 * jax.random.uniform(own_keys[10], (TEN, RANK, D), jnp.float32) ** block_levels(own_keys[10], (TEN, RANK, D), ((0, 16),), -0.2, 0.2)), 0.02, 0.2)
    return dict(features=features, cotangent=cotangent, token_tenant=token_tenant, owner_device=owner_device, frozen_weight=frozen_weight, adapter_down=adapter_down, adapter_up=adapter_up, momentum_down=momentum_down, momentum_up=momentum_up, variance_down=variance_down, variance_up=variance_up)


adapter_scale = 2.0
clip_norm = 12000.0
learn_rate = 0.004
beta_one = 0.9
beta_two = 0.999
adam_eps = 1e-08
correct_one = 1.0 - beta_one ** 20
correct_two = 1.0 - beta_two ** 20

def tenant_mask(token_tenant, tenants, lowrank):
    columns = lax.broadcasted_iota(jnp.int32, (1, tenants * lowrank), 1) // lowrank
    return token_tenant[:, None] == columns

def rank_fold(tenants, lowrank):
    row_index = lax.broadcasted_iota(jnp.int32, (tenants * lowrank, lowrank), 0) % lowrank
    col_index = lax.broadcasted_iota(jnp.int32, (tenants * lowrank, lowrank), 1)
    return (row_index == col_index).astype(jnp.float32)

def select_rank(scores, token_mask, folding):
    picked = jnp.where(token_mask, scores, jnp.zeros_like(scores))
    return jnp.dot(picked, folding, precision=lax.Precision.HIGHEST, preferred_element_type=jnp.float32)

def spread_rank(values, token_mask, tenants):
    scaled = (adapter_scale * values).astype(jnp.bfloat16)
    tiled_rank = jnp.tile(scaled, (1, tenants))
    return jnp.where(token_mask, tiled_rank, jnp.zeros_like(tiled_rank))

def owner_order(owner_device):
    total = owner_device.shape[0]
    slot_index = lax.broadcasted_iota(jnp.int32, (total, total), 0)
    tenant_index = lax.broadcasted_iota(jnp.int32, (total, total), 1)
    return lax.optimization_barrier(jnp.sum(jnp.where(owner_device[None, :] == slot_index, tenant_index, 0), axis=1)).astype(jnp.int32)

def adam_step(gradient, factor, moment, square):
    clipped = gradient * factor
    moment_next = beta_one * moment + (1.0 - beta_one) * clipped
    square_next = beta_two * square + (1.0 - beta_two) * clipped * clipped
    change = learn_rate * (moment_next / correct_one) / (jnp.sqrt(square_next / correct_two) + adam_eps)
    return (moment_next, square_next, change)

def reference(features, cotangent, token_tenant, owner_device, frozen_weight, adapter_down, adapter_up, momentum_down, momentum_up, variance_down, variance_up):
    tenants, lowrank, width = adapter_down.shape
    token_mask = tenant_mask(token_tenant, tenants, lowrank)
    folding = rank_fold(tenants, lowrank)
    down_flat = adapter_down.reshape(tenants * lowrank, width)
    up_flattened = adapter_up.reshape(tenants * lowrank, width)
    contract = (((1,), (1,)), ((), ()))
    down_sum = select_rank(lax.dot_general(features, down_flat, contract, preferred_element_type=jnp.float32), token_mask, folding)
    up_sum = select_rank(lax.dot_general(cotangent, up_flattened, contract, preferred_element_type=jnp.float32), token_mask, folding)
    frozen_result = jnp.dot(features, frozen_weight, preferred_element_type=jnp.float32)
    down_scattered = spread_rank(down_sum, token_mask, tenants)
    up_scattered = spread_rank(up_sum, token_mask, tenants)
    adapter_result = jnp.dot(down_scattered, up_flattened, preferred_element_type=jnp.float32)
    projected = (frozen_result + adapter_result).astype(jnp.bfloat16)
    outer_product = (((0,), (0,)), ((), ()))
    down_gradient = lax.dot_general(up_scattered, features, outer_product, preferred_element_type=jnp.float32)
    up_gradient = lax.dot_general(down_scattered, cotangent, outer_product, preferred_element_type=jnp.float32)
    down_gradient = down_gradient.reshape(tenants, lowrank, width)
    up_gradient = up_gradient.reshape(tenants, lowrank, width)
    slot_tenant = owner_order(owner_device)
    own_down = jnp.take(down_gradient, slot_tenant, axis=0)
    own_up = jnp.take(up_gradient, slot_tenant, axis=0)
    squares = lax.optimization_barrier(jnp.sum(own_down * own_down, axis=(1, 2))) + lax.optimization_barrier(jnp.sum(own_up * own_up, axis=(1, 2)))
    factor = (clip_norm / jnp.maximum(jnp.sqrt(squares), clip_norm))[:, None, None]
    mean_down, power_down, change_down = adam_step(own_down, factor, momentum_down, variance_down)
    mean_up, power_up, change_up = adam_step(own_up, factor, momentum_up, variance_up)
    back_down = jnp.take(change_down, owner_device, axis=0)
    back_up = jnp.take(change_up, owner_device, axis=0)
    updated_down = (adapter_down.astype(jnp.float32) - back_down).astype(jnp.bfloat16)
    updated_up = (adapter_up.astype(jnp.float32) - back_up).astype(jnp.bfloat16)
    return (projected, updated_down, updated_up, mean_down, mean_up, power_down, power_up)
```

```python
import functools

import jax
import jax.numpy as jnp
from jax import lax
from jax.experimental import pallas as pl
from jax.experimental.pallas import tpu as pltpu
from jax.sharding import PartitionSpec as P

MESH = pl.DeviceIdType.MESH

adapter_scale = 2.0
clip_norm = 12000.0
learn_rate = 0.004
beta_one = 0.9
beta_two = 0.999
adam_eps = 1e-08
correct_one = 1.0 - beta_one**20
correct_two = 1.0 - beta_two**20

EARLY_PAIR = 1
EARLY_LINE = 1


def adam_step(gradient, factor, moment, square):
    clipped = gradient * factor
    moment_next = beta_one * moment + (1.0 - beta_one) * clipped
    square_next = beta_two * square + (1.0 - beta_two) * clipped * clipped
    change = (
        learn_rate * (moment_next / correct_one) / (jnp.sqrt(square_next / correct_two) + adam_eps)
    )
    return (moment_next, square_next, change)


def line_order(line):
    order = []
    for near in range((line + 1) // 2):
        order.append(line - 1 - near)
        if near != line - 1 - near:
            order.append(near)
    return order


def kernel(
    n,
    owner_ref,
    tenant_ref,
    feat_ref,
    cot_ref,
    down_ref,
    up_ref,
    weight_ref,
    mom_down_ref,
    mom_up_ref,
    var_down_ref,
    var_up_ref,
    proj_ref,
    new_down_ref,
    new_up_ref,
    mean_down_ref,
    mean_up_ref,
    power_down_ref,
    power_up_ref,
    wbuf,
    state,
    rpart,
    rbuf,
    gsend,
    grecv,
    summed,
    owned,
    change,
    changes,
    ysend,
    yrecv,
    part,
    going_up,
    going_down,
    adapted,
    wsem,
    msem,
    rank_s,
    rank_r,
    g_s,
    g_r,
    a_s,
    a_r,
    c_s,
    c_r,
    f_s,
    f_r,
    y_s,
    y_r,
    z_s,
    u_r,
    d_r,
):
    tenants, lowrank, w = down_ref.shape
    tokens, depth = feat_ref.shape
    line = n // 2
    order = line_order(line)
    t = lax.axis_index("tensor")
    d = lax.axis_index("dp")
    zi, yi = t // 2, lax.rem(t, 2)
    mate = {"dp": 1 - d}
    pair = {"tensor": zi * 2 + 1 - yi}

    def peer(o):
        return lax.rem(t + o, n)

    def columns(block):
        return pl.ds(pl.multiple_of(block * w, w), w)

    barrier = pltpu.get_barrier_semaphore()

    @pl.loop(1, n)
    def _(o):
        pl.semaphore_signal(barrier, inc=1, device_id={"tensor": peer(o)}, device_id_type=MESH)

    pl.semaphore_signal(barrier, inc=1, device_id=mate, device_id_type=MESH)

    def weight_copy(i, block):
        return pltpu.make_async_copy(
            weight_ref.at[:, columns(block)], wbuf.at[i], wsem.at[i]
        )

    blocks = [z * 2 + 1 - yi for z in order] + [z * 2 + yi for z in order]
    for i, block in enumerate(blocks):
        weight_copy(i, block).start()
    state_copies = [
        pltpu.make_async_copy(ref, state.at[i], msem.at[i])
        for i, ref in enumerate((mom_down_ref, mom_up_ref, var_down_ref, var_up_ref))
    ]
    for copy in state_copies:
        copy.start()

    tenant = tenant_ref[...]
    contract = (((1,), (1,)), ((), ()))
    tenant_row = lax.broadcasted_iota(jnp.int32, (tenants, lowrank, tokens), 0)
    tenant_hit = tenant_row == tenant[None]

    def rank_part(adapter, rows):
        scores = lax.dot_general(
            adapter[...].reshape(tenants * lowrank, w),
            rows[...],
            contract,
            preferred_element_type=jnp.float32,
        ).reshape(tenants, lowrank, tokens)
        return jnp.sum(jnp.where(tenant_hit, scores, 0.0), axis=0)

    rpart[0] = rank_part(down_ref, feat_ref)
    rpart[1] = rank_part(up_ref, cot_ref)

    pl.semaphore_wait(barrier, n)

    def rank_copy(o, source):
        return pltpu.make_async_remote_copy(
            src_ref=rpart,
            dst_ref=rbuf.at[source],
            send_sem=rank_s.at[o],
            recv_sem=rank_r.at[source],
            device_id={"tensor": peer(o)},
            device_id_type=MESH,
        )

    @pl.loop(1, n)
    def _(o):
        rank_copy(o, t).start()

    def pair_copy(z):
        return pltpu.make_async_remote_copy(
            src_ref=ysend.at[z],
            dst_ref=yrecv.at[z],
            send_sem=y_s.at[z],
            recv_sem=y_r.at[z],
            device_id=pair,
            device_id_type=MESH,
        )

    def frozen(i, block):
        weight_copy(i, block).wait()
        return jnp.dot(feat_ref[...], wbuf[i], preferred_element_type=jnp.float32)

    for i, z in enumerate(order):
        ysend[z] = frozen(i, blocks[i])
        if i < EARLY_PAIR:
            pair_copy(z).start()

    slot = jnp.zeros_like(tenant)
    slot = lax.fori_loop(
        0, tenants, lambda k, s: jnp.where(tenant == k, owner_ref[k], s), slot
    )

    @pl.loop(1, n)
    def _(o):
        rank_copy(o, peer(o)).wait_recv()

    rbuf[t] = rpart[...]
    total = rbuf[0]
    for source in range(1, n):
        total = total + rbuf[source]
    low = adapter_scale * total
    down_low = low[0].astype(jnp.bfloat16).astype(jnp.float32)
    up_low = low[1].astype(jnp.bfloat16).astype(jnp.float32)

    half_row = lax.broadcasted_iota(jnp.int32, (n, lowrank, tokens), 0) * 2

    def half_grads(side):
        hit = half_row + side == slot[None]

        def one(values, rows):
            spread = jnp.where(hit, values[None], 0.0).reshape(n * lowrank, tokens)
            return jnp.dot(
                spread.astype(jnp.bfloat16), rows[...], preferred_element_type=jnp.float32
            ).reshape(n, lowrank, w)

        return one(up_low, feat_ref), one(down_low, cot_ref)

    def mate_copy(i):
        return pltpu.make_async_remote_copy(
            src_ref=gsend.at[i],
            dst_ref=grecv.at[i],
            send_sem=g_s.at[i],
            recv_sem=g_r.at[i],
            device_id=mate,
            device_id_type=MESH,
        )

    theirs = half_grads(1 - d)
    for i in range(2):
        gsend[i] = theirs[i]
    for i in range(2):
        mate_copy(i).start()
    mine = half_grads(d)
    for i in range(2):
        summed[:, i] = mine[i]
    for i in range(2):
        mate_copy(i).wait_recv()
        summed[:, i] = summed[:, i] + grecv[i]

    def grad_copy(o, source):
        return pltpu.make_async_remote_copy(
            src_ref=summed.at[peer(o)],
            dst_ref=owned.at[source],
            send_sem=a_s.at[o],
            recv_sem=a_r.at[source],
            device_id={"tensor": peer(o)},
            device_id_type=MESH,
        )

    @pl.loop(1, n)
    def _(o):
        grad_copy(o, t).start()

    for z in order[EARLY_PAIR:]:
        pair_copy(z).start()

    owned[t] = summed[t]

    down_spread = jnp.where(tenant_hit, down_low[None], 0.0).reshape(tenants * lowrank, tokens)
    adapted[...] = jnp.dot(
        jnp.transpose(down_spread).astype(jnp.bfloat16),
        up_ref[...].reshape(tenants * lowrank, w),
        preferred_element_type=jnp.float32,
    )
    for i, z in enumerate(order):
        part[z] = frozen(line + i, blocks[line + i])

    def up_copy(z):
        return pltpu.make_async_remote_copy(
            src_ref=part.at[z],
            dst_ref=going_up.at[z],
            send_sem=z_s.at[z],
            recv_sem=u_r.at[z],
            device_id={"tensor": lax.rem(t + 2, n)},
            device_id_type=MESH,
        )

    def down_copy(z):
        return pltpu.make_async_remote_copy(
            src_ref=part.at[z],
            dst_ref=going_down.at[z],
            send_sem=z_s.at[z],
            recv_sem=d_r.at[z],
            device_id={"tensor": lax.rem(t + n - 2, n)},
            device_id_type=MESH,
        )

    def pair_sum(z):
        pair_copy(z).wait_recv()
        part[z] = part[z] + yrecv[z]

    def ends(z):
        @pl.when(jnp.logical_and(zi == 0, z > 0))
        def _():
            up_copy(z).start()

        @pl.when(jnp.logical_and(zi == line - 1, z < line - 1))
        def _():
            down_copy(z).start()

    def middles(z):
        @pl.when(jnp.logical_and(zi > 0, zi < z))
        def _():
            up_copy(z).wait_recv()
            part[z] = part[z] + going_up[z]
            up_copy(z).start()

        @pl.when(jnp.logical_and(zi > z, zi < line - 1))
        def _():
            down_copy(z).wait_recv()
            part[z] = part[z] + going_down[z]
            down_copy(z).start()

    for z in order[:EARLY_LINE]:
        pair_sum(z)
        ends(z)

    for copy in state_copies:
        copy.wait()

    @pl.loop(1, n)
    def _(o):
        grad_copy(o, peer(o)).wait_recv()

    def squares_of(k, acc):
        g = owned[k]
        return acc + jnp.sum(g * g, axis=0)

    squares = lax.fori_loop(0, n, squares_of, jnp.zeros((lowrank, w), jnp.float32))
    squares = jnp.sum(squares, axis=(0, 1), keepdims=True)
    factor = clip_norm / jnp.maximum(jnp.sqrt(squares), clip_norm)

    def change_copy(o, source):
        return pltpu.make_async_remote_copy(
            src_ref=change.at[peer(o)],
            dst_ref=changes.at[source * 2 + d],
            send_sem=c_s.at[o],
            recv_sem=c_r.at[source],
            device_id={"tensor": peer(o)},
            device_id_type=MESH,
        )

    def step_piece(k):
        at = columns(k)
        for i, (mean_ref, power_ref) in enumerate(
            ((mean_down_ref, power_down_ref), (mean_up_ref, power_up_ref))
        ):
            mean, power, moved = adam_step(
                owned[k, i], factor, state[i, 0, :, at], state[2 + i, 0, :, at]
            )
            mean_ref[0, :, at] = mean
            power_ref[0, :, at] = power
            change[k, i] = moved

    @pl.loop(1, n)
    def _(o):
        step_piece(peer(o))

        @pl.when(o > 1)
        def _():
            change_copy(o - 1, t).start()

    step_piece(t)
    change_copy(n - 1, t).start()
    changes[t * 2 + d] = change[t]

    for z in order[EARLY_LINE:]:
        pair_sum(z)
        ends(z)

    def forward_copy(source, side):
        at = source * 2 + side
        return pltpu.make_async_remote_copy(
            src_ref=changes.at[at],
            dst_ref=changes.at[at],
            send_sem=f_s.at[source],
            recv_sem=f_r.at[source],
            device_id=mate,
            device_id_type=MESH,
        )

    forward_copy(t, d).start()
    for z in order:
        middles(z)

    @pl.loop(1, n)
    def _(o):
        change_copy(o, peer(n - o)).wait_recv()
        forward_copy(peer(n - o), d).start()

    @pl.when(zi > 0)
    def _():
        up_copy(zi).wait_recv()
        part[zi] = part[zi] + going_up[zi]

    @pl.when(zi < line - 1)
    def _():
        down_copy(zi).wait_recv()
        part[zi] = part[zi] + going_down[zi]

    proj_ref[...] = (part[zi] + adapted[...]).astype(proj_ref.dtype)

    @pl.loop(0, n)
    def _(source):
        forward_copy(source, 1 - d).wait_recv()

    @pl.loop(0, tenants)
    def _(k):
        back = changes[owner_ref[k]]
        new_down_ref[k] = (down_ref[k].astype(jnp.float32) - back[0]).astype(jnp.bfloat16)
        new_up_ref[k] = (up_ref[k].astype(jnp.float32) - back[1]).astype(jnp.bfloat16)

    @pl.loop(1, n)
    def _(o):
        rank_copy(o, t).wait_send()
        grad_copy(o, t).wait_send()
        change_copy(o, t).wait_send()

    @pl.loop(0, n)
    def _(source):
        forward_copy(source, d).wait_send()

    for i in range(2):
        mate_copy(i).wait_send()
    for z in order:
        pair_copy(z).wait_send()

        @pl.when(zi != z)
        def _():
            up_copy(z).wait_send()


def on_device(n, *args):
    (
        features,
        cotangent,
        token_tenant,
        owner_device,
        frozen_weight,
        adapter_down,
        adapter_up,
        momentum_down,
        momentum_up,
        variance_down,
        variance_up,
    ) = args
    tokens, depth = features.shape
    tenants, lowrank, w = adapter_down.shape
    line = n // 2
    f32 = jnp.float32
    vmem = pl.BlockSpec(memory_space=pltpu.VMEM)
    hbm = pl.BlockSpec(memory_space=pl.ANY)
    dma = pltpu.SemaphoreType.DMA
    shape = jax.ShapeDtypeStruct
    return pl.pallas_call(
        functools.partial(kernel, n),
        out_shape=(
            shape((tokens, w), jnp.bfloat16),
            shape(adapter_down.shape, jnp.bfloat16),
            shape(adapter_up.shape, jnp.bfloat16),
            shape(momentum_down.shape, f32),
            shape(momentum_up.shape, f32),
            shape(variance_down.shape, f32),
            shape(variance_up.shape, f32),
        ),
        in_specs=[pl.BlockSpec(memory_space=pltpu.SMEM)] + [vmem] * 5 + [hbm] * 5,
        out_specs=[vmem] * 7,
        scratch_shapes=[
            pltpu.VMEM((n, depth, w), jnp.bfloat16),
            pltpu.VMEM((4,) + momentum_down.shape, f32),
            pltpu.VMEM((2, lowrank, tokens), f32),
            pltpu.VMEM((n, 2, lowrank, tokens), f32),
            pltpu.VMEM((2, n, lowrank, w), f32),
            pltpu.VMEM((2, n, lowrank, w), f32),
            pltpu.VMEM((n, 2, lowrank, w), f32),
            pltpu.VMEM((n, 2, lowrank, w), f32),
            pltpu.VMEM((n, 2, lowrank, w), f32),
            pltpu.VMEM((tenants, 2, lowrank, w), f32),
            pltpu.VMEM((line, tokens, w), f32),
            pltpu.VMEM((line, tokens, w), f32),
            pltpu.VMEM((line, tokens, w), f32),
            pltpu.VMEM((line, tokens, w), f32),
            pltpu.VMEM((line, tokens, w), f32),
            pltpu.VMEM((tokens, w), f32),
            dma((n,)),
            dma((4,)),
            dma((n,)),
            dma((n,)),
            dma((2,)),
            dma((2,)),
            dma((n,)),
            dma((n,)),
            dma((n,)),
            dma((n,)),
            dma((n,)),
            dma((n,)),
            dma((line,)),
            dma((line,)),
            dma((line,)),
            dma((line,)),
            dma((line,)),
        ],
        compiler_params=pltpu.CompilerParams(
            collective_id=0, has_side_effects=True, vmem_limit_bytes=60 * 1024 * 1024
        ),
    )(
        owner_device,
        token_tenant.reshape(1, tokens),
        features,
        cotangent,
        adapter_down,
        adapter_up,
        frozen_weight,
        momentum_down,
        momentum_up,
        variance_down,
        variance_up,
    )


def solution(mesh):
    in_specs = (
        P(("group", "dp"), "tensor"),
        P(("group", "dp"), "tensor"),
        P(("group", "dp")),
        P("group"),
        P("tensor", None),
        P("group", None, "tensor"),
        P("group", None, "tensor"),
        P(("group", "tensor", "dp"), None, None),
        P(("group", "tensor", "dp"), None, None),
        P(("group", "tensor", "dp"), None, None),
        P(("group", "tensor", "dp"), None, None),
    )
    out_specs = (
        P(("group", "dp"), "tensor"),
        P("group", None, "tensor"),
        P("group", None, "tensor"),
        P(("group", "tensor", "dp"), None, None),
        P(("group", "tensor", "dp"), None, None),
        P(("group", "tensor", "dp"), None, None),
        P(("group", "tensor", "dp"), None, None),
    )
    return jax.shard_map(
        functools.partial(on_device, mesh.shape["tensor"]),
        mesh=mesh,
        in_specs=in_specs,
        out_specs=out_specs,
        check_vma=False,
    )
```

```python
import functools

import jax
import jax.numpy as jnp
from jax import lax
from jax.experimental import pallas as pl
from jax.experimental.pallas import tpu as pltpu
from jax.sharding import PartitionSpec as P

MESH = pl.DeviceIdType.MESH

adapter_scale = 2.0
clip_norm = 12000.0
learn_rate = 0.004
beta_one = 0.9
beta_two = 0.999
adam_eps = 1e-08
correct_one = 1.0 - beta_one**20
correct_two = 1.0 - beta_two**20

CHUNKS = 2


def adam_step(gradient, factor, moment, square):
    clipped = gradient * factor
    moment_next = beta_one * moment + (1.0 - beta_one) * clipped
    square_next = beta_two * square + (1.0 - beta_two) * clipped * clipped
    change = (
        learn_rate * (moment_next / correct_one) / (jnp.sqrt(square_next / correct_two) + adam_eps)
    )
    return (moment_next, square_next, change)


def line_order(line):
    order = []
    for near in range((line + 1) // 2):
        order.append(line - 1 - near)
        if near != line - 1 - near:
            order.append(near)
    return order


def kernel(
    n,
    owner_ref,
    tenant_ref,
    feat_ref,
    cot_ref,
    down_ref,
    up_ref,
    weight_ref,
    mom_down_ref,
    mom_up_ref,
    var_down_ref,
    var_up_ref,
    proj_ref,
    new_down_ref,
    new_up_ref,
    mean_down_ref,
    mean_up_ref,
    power_down_ref,
    power_up_ref,
    wbuf,
    state,
    rpart,
    rbuf,
    gsend,
    grecv,
    summed,
    owned,
    change,
    changes,
    ysend,
    yrecv,
    part,
    going_up,
    going_down,
    adapted,
    wsem,
    msem,
    rank_s,
    rank_r,
    g_s,
    g_r,
    a_s,
    a_r,
    c_s,
    c_r,
    f_s,
    f_r,
    y_s,
    y_r,
    z_s,
    u_r,
    d_r,
):
    tenants, lowrank, w = down_ref.shape
    tokens, depth = feat_ref.shape
    line = n // 2
    order = line_order(line)
    t = lax.axis_index("tensor")
    d = lax.axis_index("dp")
    zi, yi = t // 2, lax.rem(t, 2)
    mate = {"dp": 1 - d}
    pair = {"tensor": zi * 2 + 1 - yi}

    quarter = max(1, line // 4)
    waves = (
        order[:quarter],
        order[quarter : 2 * quarter],
        order[2 * quarter : 3 * quarter],
        order[3 * quarter :],
    )
    height = tokens // CHUNKS
    paired = n & (n - 1) == 0

    def peer(o):
        return t ^ (n - o) if paired else lax.rem(t + o, n)

    def giver(o):
        return t ^ (n - o) if paired else lax.rem(t + n - o, n)

    def columns(block):
        return pl.ds(pl.multiple_of(block * w, w), w)

    barrier = pltpu.get_barrier_semaphore()

    @pl.loop(1, n)
    def _(o):
        pl.semaphore_signal(barrier, inc=1, device_id={"tensor": peer(o)}, device_id_type=MESH)

    pl.semaphore_signal(barrier, inc=1, device_id=mate, device_id_type=MESH)

    def weight_copy(i, block):
        return pltpu.make_async_copy(
            weight_ref.at[:, columns(block)], wbuf.at[i], wsem.at[i]
        )

    blocks = [z * 2 + 1 - yi for z in order] + [z * 2 + yi for z in order]
    for i, block in enumerate(blocks):
        weight_copy(i, block).start()
    state_copies = [
        pltpu.make_async_copy(ref, state.at[i], msem.at[i])
        for i, ref in enumerate((mom_down_ref, mom_up_ref, var_down_ref, var_up_ref))
    ]
    for copy in state_copies:
        copy.start()

    tenant = tenant_ref[...]
    contract = (((1,), (1,)), ((), ()))
    tenant_row = lax.broadcasted_iota(jnp.int32, (tenants, lowrank, tokens), 0)
    tenant_hit = tenant_row == tenant[None]

    def rank_part(adapter, rows):
        scores = lax.dot_general(
            adapter[...].reshape(tenants * lowrank, w),
            rows[...],
            contract,
            preferred_element_type=jnp.float32,
        ).reshape(tenants, lowrank, tokens)
        return jnp.sum(jnp.where(tenant_hit, scores, 0.0), axis=0)

    rpart[0] = rank_part(down_ref, feat_ref)
    rpart[1] = rank_part(up_ref, cot_ref)

    pl.semaphore_wait(barrier, n)

    def rank_copy(o, source):
        return pltpu.make_async_remote_copy(
            src_ref=rpart,
            dst_ref=rbuf.at[source],
            send_sem=rank_s.at[o],
            recv_sem=rank_r.at[source],
            device_id={"tensor": peer(o)},
            device_id_type=MESH,
        )

    @pl.loop(1, n)
    def _(o):
        rank_copy(o, t).start()

    def rows_of(c):
        return pl.ds(c * height, height)

    def pair_copy(z, c):
        return pltpu.make_async_remote_copy(
            src_ref=ysend.at[z, rows_of(c)],
            dst_ref=yrecv.at[z, rows_of(c)],
            send_sem=y_s.at[z * CHUNKS + c],
            recv_sem=y_r.at[z * CHUNKS + c],
            device_id=pair,
            device_id_type=MESH,
        )

    def pair_start(z):
        for c in range(CHUNKS):
            pair_copy(z, c).start()

    def frozen(i, block):
        weight_copy(i, block).wait()
        return jnp.dot(feat_ref[...], wbuf[i], preferred_element_type=jnp.float32)

    for i, z in enumerate(order):
        ysend[z] = frozen(i, blocks[i])
        if z in waves[0]:
            pair_start(z)

    slot = jnp.zeros_like(tenant)
    slot = lax.fori_loop(
        0, tenants, lambda k, s: jnp.where(tenant == k, owner_ref[k], s), slot
    )

    @pl.loop(1, n)
    def _(o):
        rank_copy(o, giver(o)).wait_recv()

    rbuf[t] = rpart[...]
    total = rbuf[0]
    for source in range(1, n):
        total = total + rbuf[source]
    low = adapter_scale * total
    down_low = low[0].astype(jnp.bfloat16).astype(jnp.float32)
    up_low = low[1].astype(jnp.bfloat16).astype(jnp.float32)

    half_row = lax.broadcasted_iota(jnp.int32, (n, lowrank, tokens), 0) * 2

    def half_grads(side):
        hit = half_row + side == slot[None]

        def one(values, rows):
            spread = jnp.where(hit, values[None], 0.0).reshape(n * lowrank, tokens)
            return jnp.dot(
                spread.astype(jnp.bfloat16), rows[...], preferred_element_type=jnp.float32
            ).reshape(n, lowrank, w)

        return one(up_low, feat_ref), one(down_low, cot_ref)

    def mate_copy(i):
        return pltpu.make_async_remote_copy(
            src_ref=gsend.at[i],
            dst_ref=grecv.at[i],
            send_sem=g_s.at[i],
            recv_sem=g_r.at[i],
            device_id=mate,
            device_id_type=MESH,
        )

    theirs = half_grads(1 - d)
    for i in range(2):
        gsend[i] = theirs[i]
    for i in range(2):
        mate_copy(i).start()
    mine = half_grads(d)
    for i in range(2):
        summed[:, i] = mine[i]
    for i in range(2):
        mate_copy(i).wait_recv()
        summed[:, i] = summed[:, i] + grecv[i]

    def grad_copy(o, source):
        return pltpu.make_async_remote_copy(
            src_ref=summed.at[peer(o)],
            dst_ref=owned.at[source],
            send_sem=a_s.at[o],
            recv_sem=a_r.at[source],
            device_id={"tensor": peer(o)},
            device_id_type=MESH,
        )

    @pl.loop(1, n)
    def _(o):
        grad_copy(o, t).start()

    for z in waves[1]:
        pair_start(z)

    owned[t] = summed[t]

    down_spread = jnp.where(tenant_hit, down_low[None], 0.0).reshape(tenants * lowrank, tokens)
    adapted[...] = jnp.dot(
        jnp.transpose(down_spread).astype(jnp.bfloat16),
        up_ref[...].reshape(tenants * lowrank, w),
        preferred_element_type=jnp.float32,
    )
    for i, z in enumerate(order):
        part[z] = frozen(line + i, blocks[line + i])

    def up_copy(z, c):
        return pltpu.make_async_remote_copy(
            src_ref=part.at[z, rows_of(c)],
            dst_ref=going_up.at[z, rows_of(c)],
            send_sem=z_s.at[z * CHUNKS + c],
            recv_sem=u_r.at[z * CHUNKS + c],
            device_id={"tensor": lax.rem(t + 2, n)},
            device_id_type=MESH,
        )

    def down_copy(z, c):
        return pltpu.make_async_remote_copy(
            src_ref=part.at[z, rows_of(c)],
            dst_ref=going_down.at[z, rows_of(c)],
            send_sem=z_s.at[z * CHUNKS + c],
            recv_sem=d_r.at[z * CHUNKS + c],
            device_id={"tensor": lax.rem(t + n - 2, n)},
            device_id_type=MESH,
        )

    def ends(z):
        for c in range(CHUNKS):
            at = rows_of(c)
            pair_copy(z, c).wait_recv()
            part[z, at] = part[z, at] + yrecv[z, at]

            @pl.when(jnp.logical_and(zi == 0, z > 0))
            def _():
                up_copy(z, c).start()

            @pl.when(jnp.logical_and(zi == line - 1, z < line - 1))
            def _():
                down_copy(z, c).start()

    def middles(z):
        for c in range(CHUNKS):
            at = rows_of(c)

            @pl.when(jnp.logical_and(zi > 0, zi < z))
            def _():
                up_copy(z, c).wait_recv()
                part[z, at] = part[z, at] + going_up[z, at]
                up_copy(z, c).start()

            @pl.when(jnp.logical_and(zi > z, zi < line - 1))
            def _():
                down_copy(z, c).wait_recv()
                part[z, at] = part[z, at] + going_down[z, at]
                down_copy(z, c).start()

    for z in waves[0]:
        ends(z)

    for copy in state_copies:
        copy.wait()

    @pl.loop(1, n)
    def _(o):
        grad_copy(o, giver(o)).wait_recv()

    for z in waves[2]:
        pair_start(z)

    def squares_of(k, acc):
        g = owned[k]
        return acc + jnp.sum(g * g, axis=0)

    squares = lax.fori_loop(0, n, squares_of, jnp.zeros((lowrank, w), jnp.float32))
    squares = jnp.sum(squares, axis=(0, 1), keepdims=True)
    factor = clip_norm / jnp.maximum(jnp.sqrt(squares), clip_norm)

    def change_copy(o, source):
        return pltpu.make_async_remote_copy(
            src_ref=change.at[peer(o)],
            dst_ref=changes.at[source * 2 + d],
            send_sem=c_s.at[o],
            recv_sem=c_r.at[source],
            device_id={"tensor": peer(o)},
            device_id_type=MESH,
        )

    def step_piece(k):
        at = columns(k)
        for i in range(2):
            mean, power, moved = adam_step(
                owned[k, i], factor, state[i, 0, :, at], state[2 + i, 0, :, at]
            )
            state[i, 0, :, at] = mean
            state[2 + i, 0, :, at] = power
            change[k, i] = moved

    @pl.loop(1, n)
    def _(o):
        step_piece(peer(o))

        @pl.when(o > 1)
        def _():
            change_copy(o - 1, t).start()

    step_piece(t)
    change_copy(n - 1, t).start()
    changes[t * 2 + d] = change[t]

    def forward_copy(source, side):
        at = source * 2 + side
        return pltpu.make_async_remote_copy(
            src_ref=changes.at[at],
            dst_ref=changes.at[at],
            send_sem=f_s.at[source],
            recv_sem=f_r.at[source],
            device_id=mate,
            device_id_type=MESH,
        )

    forward_copy(t, d).start()
    state_outs = [
        pltpu.make_async_copy(state.at[i], ref, msem.at[i])
        for i, ref in enumerate((mean_down_ref, mean_up_ref, power_down_ref, power_up_ref))
    ]
    for copy in state_outs:
        copy.start()

    for z in waves[3]:
        pair_start(z)
    for z in waves[1]:
        ends(z)
    for z in waves[0]:
        middles(z)
    for z in waves[2]:
        ends(z)

    @pl.loop(1, n)
    def _(o):
        change_copy(o, giver(o)).wait_recv()
        forward_copy(giver(o), d).start()

    for z in waves[3]:
        ends(z)
    for z in waves[1] + waves[2]:
        middles(z)

    @pl.loop(0, n)
    def _(source):
        forward_copy(source, 1 - d).wait_recv()

    @pl.loop(0, tenants)
    def _(k):
        back = changes[owner_ref[k]]
        new_down_ref[k] = (down_ref[k].astype(jnp.float32) - back[0]).astype(jnp.bfloat16)
        new_up_ref[k] = (up_ref[k].astype(jnp.float32) - back[1]).astype(jnp.bfloat16)

    for z in waves[3]:
        middles(z)

    for c in range(CHUNKS):
        at = rows_of(c)

        @pl.when(zi > 0)
        def _():
            up_copy(zi, c).wait_recv()
            part[zi, at] = part[zi, at] + going_up[zi, at]

        @pl.when(zi < line - 1)
        def _():
            down_copy(zi, c).wait_recv()
            part[zi, at] = part[zi, at] + going_down[zi, at]

        proj_ref[at] = (part[zi, at] + adapted[at]).astype(proj_ref.dtype)

    for copy in state_outs:
        copy.wait()

    @pl.loop(1, n)
    def _(o):
        rank_copy(o, t).wait_send()
        grad_copy(o, t).wait_send()
        change_copy(o, t).wait_send()

    @pl.loop(0, n)
    def _(source):
        forward_copy(source, d).wait_send()

    for i in range(2):
        mate_copy(i).wait_send()
    for z in order:
        for c in range(CHUNKS):
            pair_copy(z, c).wait_send()

            @pl.when(zi != z)
            def _():
                up_copy(z, c).wait_send()


def hand_out(*refs):
    count = len(refs) // 3
    sources, results, held = refs[:count], refs[count : 2 * count], refs[2 * count : 3 * count]
    sems = refs[-1]
    ins = [pltpu.make_async_copy(sources[i], held[i], sems.at[0, i]) for i in range(count)]
    outs = [pltpu.make_async_copy(held[i], results[i], sems.at[1, i]) for i in range(count)]
    for copy in ins:
        copy.start()
    for i in range(count):
        ins[i].wait()
        outs[i].start()
    for copy in outs:
        copy.wait()


def on_device(n, *args):
    (
        features,
        cotangent,
        token_tenant,
        owner_device,
        frozen_weight,
        adapter_down,
        adapter_up,
        momentum_down,
        momentum_up,
        variance_down,
        variance_up,
    ) = args
    tokens, depth = features.shape
    tenants, lowrank, w = adapter_down.shape
    line = n // 2
    f32 = jnp.float32
    vmem = pl.BlockSpec(memory_space=pltpu.VMEM)
    hbm = pl.BlockSpec(memory_space=pl.ANY)
    dma = pltpu.SemaphoreType.DMA
    shape = jax.ShapeDtypeStruct
    results = pl.pallas_call(
        functools.partial(kernel, n),
        out_shape=(
            shape((tokens, w), jnp.bfloat16),
            shape(adapter_down.shape, jnp.bfloat16),
            shape(adapter_up.shape, jnp.bfloat16),
            shape(momentum_down.shape, f32),
            shape(momentum_up.shape, f32),
            shape(variance_down.shape, f32),
            shape(variance_up.shape, f32),
        ),
        in_specs=[pl.BlockSpec(memory_space=pltpu.SMEM)] + [vmem] * 5 + [hbm] * 5,
        out_specs=[vmem] * 3 + [hbm] * 4,
        scratch_shapes=[
            pltpu.VMEM((n, depth, w), jnp.bfloat16),
            pltpu.VMEM((4,) + momentum_down.shape, f32),
            pltpu.VMEM((2, lowrank, tokens), f32),
            pltpu.VMEM((n, 2, lowrank, tokens), f32),
            pltpu.VMEM((2, n, lowrank, w), f32),
            pltpu.VMEM((2, n, lowrank, w), f32),
            pltpu.VMEM((n, 2, lowrank, w), f32),
            pltpu.VMEM((n, 2, lowrank, w), f32),
            pltpu.VMEM((n, 2, lowrank, w), f32),
            pltpu.VMEM((tenants, 2, lowrank, w), f32),
            pltpu.VMEM((line, tokens, w), f32),
            pltpu.VMEM((line, tokens, w), f32),
            pltpu.VMEM((line, tokens, w), f32),
            pltpu.VMEM((line, tokens, w), f32),
            pltpu.VMEM((line, tokens, w), f32),
            pltpu.VMEM((tokens, w), f32),
            dma((n,)),
            dma((4,)),
            dma((n,)),
            dma((n,)),
            dma((2,)),
            dma((2,)),
            dma((n,)),
            dma((n,)),
            dma((n,)),
            dma((n,)),
            dma((n,)),
            dma((n,)),
            dma((line * CHUNKS,)),
            dma((line * CHUNKS,)),
            dma((line * CHUNKS,)),
            dma((line * CHUNKS,)),
            dma((line * CHUNKS,)),
        ],
        compiler_params=pltpu.CompilerParams(
            collective_id=0, has_side_effects=True, vmem_limit_bytes=60 * 1024 * 1024
        ),
    )(
        owner_device,
        token_tenant.reshape(1, tokens),
        features,
        cotangent,
        adapter_down,
        adapter_up,
        frozen_weight,
        momentum_down,
        momentum_up,
        variance_down,
        variance_up,
    )
    return pl.pallas_call(
        hand_out,
        out_shape=tuple(shape(r.shape, r.dtype) for r in results),
        in_specs=[hbm] * len(results),
        out_specs=[hbm] * len(results),
        scratch_shapes=[pltpu.VMEM(r.shape, r.dtype) for r in results]
        + [dma((2, len(results)))],
    )(*results)


def solution(mesh):
    in_specs = (
        P(("group", "dp"), "tensor"),
        P(("group", "dp"), "tensor"),
        P(("group", "dp")),
        P("group"),
        P("tensor", None),
        P("group", None, "tensor"),
        P("group", None, "tensor"),
        P(("group", "tensor", "dp"), None, None),
        P(("group", "tensor", "dp"), None, None),
        P(("group", "tensor", "dp"), None, None),
        P(("group", "tensor", "dp"), None, None),
    )
    out_specs = (
        P(("group", "dp"), "tensor"),
        P("group", None, "tensor"),
        P("group", None, "tensor"),
        P(("group", "tensor", "dp"), None, None),
        P(("group", "tensor", "dp"), None, None),
        P(("group", "tensor", "dp"), None, None),
        P(("group", "tensor", "dp"), None, None),
    )
    return jax.shard_map(
        functools.partial(on_device, mesh.shape["tensor"]),
        mesh=mesh,
        in_specs=in_specs,
        out_specs=out_specs,
        check_vma=False,
    )
```
